32 devices in a mesh: seq: 8 (over z, y), batch: 4 (over x, core).
Axes of the slice: x: 2, y: 2, z: 4, core: 2. Of those that a mesh axis runs over, the one named last changes fastest.
Arguments:
- signal: bfloat16 [4, 1024, 8192], P('batch', 'seq'), may hold values from -6 to 6
- out_grad: bfloat16 [4, 1024, 8192], P('batch', 'seq'), may hold values from -6 to 6
- residues: float32 [8, 8192], replicated, may hold values from -0.3 to 0.3
- log_rates: float32 [8, 512], replicated, as said below
Outputs:
- mixed: bfloat16 [4, 1024, 8192], P('batch', 'seq')
- grad_signal: bfloat16 [4, 1024, 8192], P('batch', 'seq')
- grad_residues: float32 [8, 8192], replicated
- grad_rates: float32 [8, 512], replicated
The draws below stay inside these ranges and needn't reach their ends.
Inputs may be any that keep to these rules, and one draw needn't show every extreme that they name: Each decay rate exp(log_rates) lies between 0.2 / 1024 and 1 / 30.
All inputs are finite; a program needn't handle non-finite values.
Results may differ from the reference program's by a relative error of at most 0.0012.
Values sent between devices are 32-bit elements; how exact they have to be, the bound alone decides.
A program may use at most 384 MiB of HBM per device.

```python
import jax
import jax.numpy as jnp
from jax import lax

D = 8192
M = 8
GROUP = 16
LEN = 1024
BATCH = 4


def draw_log_rates(key, part):
    key_coin, key_slow, key_fast = jax.random.split(key, 3)
    shape = (M, D // GROUP)
    slow_share = 0.125
    coin = jax.random.uniform(key_coin, shape, jnp.float32) < slow_share
    slow_low = jnp.log(0.2 / LEN)
    slow_high = jnp.log(2.0 / LEN)
    fast_low = jnp.log(0.01)
    fast_high = jnp.log(1.0 / 30.0)
    slow_value = slow_low + jax.random.uniform(key_slow, shape, jnp.float32) * (slow_high - slow_low)
    fast_value = fast_low + jax.random.uniform(key_fast, shape, jnp.float32) * (fast_high - fast_low)
    return jnp.where(coin, slow_value, fast_value).astype(jnp.float32)


def steps_of(rng, shape, shards, smallest, high):
    def one(position, blocks):
        draws = jax.random.uniform(jax.random.fold_in(jax.random.fold_in(rng, 6), position), (blocks,), jnp.float32, smallest / len(shards), high / len(shards))
        return jnp.repeat(jnp.exp(draws), shape[position] // blocks).reshape((-1,) + (1,) * (len(shape) - position - 1))

    loudness = one(*shards[0])
    for cut in shards[1:]:
        loudness = loudness * one(*cut)
    return loudness


def normal_values(key, extent, scale, most, cuts=(), held_as=jnp.bfloat16):
    drawn = scale * jax.random.normal(key, extent, jnp.float32)
    if cuts:
        drawn = drawn * steps_of(key, extent, cuts, -0.22, 0.18)
    return jnp.clip(drawn, -most, most).astype(held_as)


def setup_inputs(seed: int = 0) -> dict:
    splits = jax.random.split(jax.random.key(seed), 5)
    signal = normal_values(splits[0], (BATCH, LEN, D), 1.0, 6.0, ((0, 4), (1, 8)))
    out_grad = normal_values(splits[1], (BATCH, LEN, D), 1.0, 6.0, ((0, 4), (1, 8)))
    residues = normal_values(splits[2], (M, D), 0.05, 0.3, (), jnp.float32)
    log_rates = draw_log_rates(jax.random.fold_in(splits[4], 71), 0)
    return dict(signal=signal, out_grad=out_grad, residues=residues, log_rates=log_rates)


def expand(values):
    return jnp.repeat(values, GROUP, axis=1)


def reference(signal, out_grad, residues, log_rates):
    decay_rate = jnp.exp(log_rates)
    pole_values = expand(jnp.exp(-decay_rate))
    empty_state = jnp.zeros((BATCH, M, D), jnp.float32)
    empty_sum = jnp.zeros((M, D), jnp.float32)

    def forward_step(carried, rows):
        modal_state, moment, sum_residue, sum_moment = carried
        signal_row = rows[0].astype(jnp.float32)[:, None, :]
        grad_row = rows[1].astype(jnp.float32)[:, None, :]
        moment = pole_values * (moment + modal_state)
        modal_state = pole_values * modal_state + signal_row
        out_row = jnp.sum(residues * modal_state, axis=1)
        sum_residue = sum_residue + jnp.sum(grad_row * modal_state, axis=0)
        sum_moment = sum_moment + jnp.sum(grad_row * moment, axis=0)
        return (modal_state, moment, sum_residue, sum_moment), out_row.astype(jnp.bfloat16)

    rows = (jnp.swapaxes(signal, 0, 1), jnp.swapaxes(out_grad, 0, 1))
    finals, outputs = lax.scan(forward_step, (empty_state, empty_state, empty_sum, empty_sum), rows)

    def backward_step(adjoint, grad_in):
        adjoint = pole_values * adjoint + grad_in.astype(jnp.float32)[:, None, :]
        return adjoint, jnp.sum(residues * adjoint, axis=1).astype(jnp.bfloat16)

    unused, grads = lax.scan(backward_step, empty_state, rows[1], reverse=True)
    norm_factor = 1.0 / (BATCH * LEN)
    grad_residues = finals[2] * norm_factor
    grad_rates = -decay_rate * jnp.sum((residues * finals[3]).reshape(M, D // GROUP, GROUP), axis=2) * norm_factor
    return jnp.swapaxes(outputs, 0, 1), jnp.swapaxes(grads, 0, 1), grad_residues, grad_rates
```

```python
import functools

import jax
import jax.numpy as jnp
import numpy as np
from jax import lax
from jax.experimental import pallas as pl
from jax.experimental.pallas import tpu as pltpu
from jax.sharding import PartitionSpec as P

LANES = 256
F32 = jnp.float32
BF16 = jnp.bfloat16


def split(value):
    high = value.astype(BF16)
    return high, (value - high.astype(F32)).astype(BF16)


def mul(a, b):
    return jnp.dot(a, b, preferred_element_type=F32)


def twice(value, axis):
    return jnp.concatenate([value, value], axis=axis)


def exact_right(left, right):
    return mul(jnp.concatenate(split(left), axis=1), right)


def three(left, right):
    left_high, left_low = split(left)
    right_high, right_low = split(right)
    return mul(left_high, right_high) + (mul(left_low, right_high) + mul(left_high, right_low))


def own_rows(wide, modes, group):
    rows, lanes = wide.shape
    owner = lax.broadcasted_iota(jnp.int32, (modes, lanes), 1) // group
    out = wide[:modes]
    for g in range(1, rows // modes):
        out = jnp.where(owner == g, wide[g * modes : (g + 1) * modes], out)
    return out


def spread(narrow, rows, group):
    modes, lanes = narrow.shape
    owner = lax.broadcasted_iota(jnp.int32, (modes, lanes), 1) // group
    return jnp.concatenate(
        [jnp.where(owner == g, narrow, 0.0) for g in range(rows // modes)], axis=0
    )


def states_kernel(modes, group, rate_ref, x_ref, g_ref, state_ref, weighted_ref):
    length = x_ref.shape[0]
    rate = rate_ref[0]
    at = lax.broadcasted_iota(jnp.int32, (length, rate.shape[1]), 0).astype(F32)
    rising = jnp.exp(-rate * at)
    falling = jnp.exp(-rate * (length - 1.0 - at))
    for k, (table, weight, values) in enumerate(
        ((falling, length - at, x_ref[...]), (rising, at, g_ref[...]))
    ):
        left = jnp.concatenate([table.T, (weight * table).T], axis=0)
        both = exact_right(left, twice(values, 0))
        rows = table.shape[1]
        state_ref[k] = own_rows(both[:rows], modes, group)
        weighted_ref[k] = own_rows(both[rows:], modes, group)


def main_kernel(
    modes, group, rate_ref, pole_ref, gap_ref, dft_ref, inv_high_ref, inv_low_ref, angle_ref,
    x_ref, g_ref, res_ref, rates_ref, state_ref, weighted_ref, carry_ref,
    y_ref, gs_ref, gres_ref, grate_ref,
):
    length = x_ref.shape[0]
    half = length // 2
    rate = rate_ref[0]
    pole = pole_ref[0]
    gap = gap_ref[0]
    gm = rate.shape[1]
    scale = 1.0 / half
    real = gap + pole * angle_ref[0]
    imag = pole * angle_ref[1]
    inverse = 1.0 / (real * real + imag * imag)
    phi_r = real * inverse
    phi_i = -imag * inverse
    psi_r = phi_r * phi_r - phi_i * phi_i - phi_r
    psi_i = 2.0 * phi_r * phi_i - phi_i
    phi = jnp.concatenate([phi_r, phi_i], axis=0)
    phi_t = jnp.concatenate([phi_r, -phi_i], axis=0).T
    psi_t = jnp.concatenate([psi_r, -psi_i], axis=0).T
    x_hat = mul(dft_ref[...], twice(x_ref[...], 0))
    g_hat = mul(dft_ref[...], twice(g_ref[...], 0))
    res = res_ref[...]
    phi_high, phi_low = split(phi)
    res_wide = spread(res, gm, group)
    res_high, res_low = split(res_wide)
    k_hat = mul(jnp.concatenate([phi_high, phi_low], 1), twice(res_high, 0)) + mul(phi_high, res_low)
    xr, xi = x_hat[:half], x_hat[half:]
    gr, gi = g_hat[:half], g_hat[half:]
    kr, ki = k_hat[:half], k_hat[half:]
    y_hat = jnp.concatenate([kr * xr - ki * xi, kr * xi + ki * xr], axis=0)
    h_hat = jnp.concatenate([kr * gr + ki * gi, kr * gi - ki * gr], axis=0)
    lag = jnp.concatenate([gr * xr + gi * xi, gr * xi - gi * xr], axis=0) * scale
    lane_rate = rates_ref[...]
    lane_pole = jnp.exp(-lane_rate)
    whole = jnp.exp(-lane_rate * length)
    fold = 1.0 / (1.0 + whole)
    s_x, s_g = state_ref[0], state_ref[1]
    carry, adjoint = carry_ref[0], carry_ref[1]
    turned_x, turned_g = s_x * fold, s_g * fold
    carry_all = carry + turned_x
    adjoint_all = adjoint + turned_g
    at = lax.broadcasted_iota(jnp.int32, (length, gm), 0).astype(F32)
    rising = jnp.exp(-rate * (at + 1.0))
    falling = jnp.exp(-rate * (length - at))
    for table, hat, start, out in (
        (rising, y_hat, carry_all, y_ref),
        (falling, h_hat, adjoint_all, gs_ref),
    ):
        table_high, table_low = split(table)
        left_high = jnp.concatenate([inv_high_ref[...], table_high], axis=1)
        left_low = jnp.concatenate([inv_low_ref[...], table_low], axis=1)
        right = jnp.concatenate([hat, spread(res * start, gm, group)], axis=0)
        right_high, right_low = split(right)
        total = mul(left_high, right_high) + mul(left_low, right_high) + mul(left_high, right_low)
        out[...] = total.astype(BF16)
    terms = jnp.concatenate([phi_t, psi_t], axis=0)
    terms_high, terms_low = split(terms)
    lag_high, lag_low = split(lag)
    wide = mul(jnp.concatenate([terms_high, terms_low], 1), twice(lag_high, 0)) + mul(
        terms_high, lag_low
    )
    sums = own_rows(wide[:gm], modes, group) + carry_all * lane_pole * s_g
    moments = (
        own_rows(wide[gm:], modes, group)
        + lane_pole * (carry_all * weighted_ref[1] + adjoint_all * weighted_ref[0])
        + length * lane_pole * whole * (carry * adjoint - turned_x * turned_g)
    )
    gres_ref[...] = sums
    rm = -lane_rate * res * moments
    rows = lax.broadcasted_iota(jnp.int32, (LANES, 128), 0) // group
    cols = lax.broadcasted_iota(jnp.int32, (LANES, 128), 1)
    pick = jnp.where(rows == cols, 1.0, 0.0).astype(BF16)
    rm_high, rm_rest = split(rm)
    rm_low = rm_rest
    both = mul(jnp.concatenate([rm_high.astype(F32), rm_low.astype(F32)], 0).astype(BF16), pick)
    grate_ref[0] = both[:modes] + both[modes:]


def constants(length):
    half = length // 2
    omega = np.pi * (2.0 * np.arange(half) + 1.0) / length
    at = np.arange(length)
    forward = np.concatenate([np.cos(np.outer(omega, at)), -np.sin(np.outer(omega, at))], axis=0)
    lanes = np.ones((1, 128))
    angle = np.stack(
        [2.0 * np.sin(omega / 2.0)[:, None] ** 2 * lanes, np.sin(omega)[:, None] * lanes]
    )
    return forward.astype(np.float32), (forward.T / half).astype(np.float32), angle.astype(np.float32)


def local(mesh_shape, signal, out_grad, residues, log_rates):
    batch_rows, length, channels = signal.shape
    modes, groups = log_rates.shape
    group = channels // groups
    blocks = channels // LANES
    gm = LANES // group * modes
    norm = 1.0 / (batch_rows * mesh_shape["batch"] * length * mesh_shape["seq"])
    decay = jnp.exp(log_rates)
    flat = decay.T.reshape(blocks, 1, gm)
    pole = jnp.exp(-flat)
    gap = -jnp.expm1(-flat)
    lane_rate = jnp.repeat(decay, group, axis=1)
    forward, inverse, angle = constants(length)
    dft_high = jnp.asarray(forward).astype(BF16)
    dft = jnp.concatenate(
        [dft_high, (jnp.asarray(forward) - dft_high.astype(F32)).astype(BF16)], axis=1
    )
    inv_high, inv_low = split(jnp.asarray(inverse))
    angle = jnp.asarray(angle)
    peers = mesh_shape["seq"]
    me = lax.axis_index("seq")

    row_spec = pl.BlockSpec((1, 1, gm), lambda b: (b, 0, 0))
    data_spec = pl.BlockSpec((length, LANES), lambda b: (0, b))
    lane_spec = pl.BlockSpec((modes, LANES), lambda b: (0, b))
    pair_spec = pl.BlockSpec((2, modes, LANES), lambda b: (0, 0, b))

    def fixed(shape):
        return pl.BlockSpec(shape, lambda b: (0,) * len(shape))

    pair = jax.ShapeDtypeStruct((2, modes, channels), F32)
    mixed, grads, res_sum, rate_sum = [], [], 0.0, 0.0
    for row in range(batch_rows):
        x, g = signal[row], out_grad[row]
        state, weighted = pl.pallas_call(
            functools.partial(states_kernel, modes, group),
            grid=(blocks,),
            in_specs=[row_spec, data_spec, data_spec],
            out_specs=[pair_spec, pair_spec],
            out_shape=[pair, pair],
        )(flat, x, g)
        every = lax.all_gather(state, "seq")
        order = jnp.arange(peers)
        ahead = (me - 1 - order).astype(F32)[:, None, None]
        behind = (order - me - 1).astype(F32)[:, None, None]
        from_left = jnp.where(ahead >= 0, jnp.exp(-lane_rate * (jnp.maximum(ahead, 0) * length)), 0.0)
        from_right = jnp.where(behind >= 0, jnp.exp(-lane_rate * (jnp.maximum(behind, 0) * length)), 0.0)
        carry = jnp.stack(
            [jnp.sum(from_left * every[:, 0], axis=0), jnp.sum(from_right * every[:, 1], axis=0)]
        )
        y, gs, part, rates = pl.pallas_call(
            functools.partial(main_kernel, modes, group),
            grid=(blocks,),
            in_specs=[
                row_spec, row_spec, row_spec,
                fixed(dft.shape), fixed(inv_high.shape), fixed(inv_low.shape), fixed(angle.shape),
                data_spec, data_spec, lane_spec, lane_spec, pair_spec, pair_spec, pair_spec,
            ],
            out_specs=[
                data_spec, data_spec, lane_spec,
                pl.BlockSpec((1, modes, 128), lambda b: (b, 0, 0)),
            ],
            out_shape=[
                jax.ShapeDtypeStruct((length, channels), BF16),
                jax.ShapeDtypeStruct((length, channels), BF16),
                jax.ShapeDtypeStruct((modes, channels), F32),
                jax.ShapeDtypeStruct((blocks, modes, 128), F32),
            ],
        )(flat, pole, gap, dft, inv_high, inv_low, angle, x, g, residues, lane_rate, state, weighted, carry)
        mixed.append(y)
        grads.append(gs)
        res_sum = res_sum + part
        rate_sum = rate_sum + rates
    rate_sum = rate_sum[:, :, : LANES // group]
    res_sum, rate_sum = lax.psum((res_sum * norm, rate_sum * norm), ("seq", "batch"))
    grad_rates = jnp.swapaxes(rate_sum, 0, 1).reshape(modes, groups)
    return jnp.stack(mixed), jnp.stack(grads), res_sum, grad_rates


def solution(mesh):
    placed = (P("batch", "seq", None), P("batch", "seq", None), P(), P())
    return jax.shard_map(
        functools.partial(local, dict(mesh.shape)),
        mesh=mesh,
        in_specs=placed,
        out_specs=placed,
        check_vma=False,
    )
```

```python
import functools

import jax
import jax.numpy as jnp
import numpy as np
from jax import lax
from jax.experimental import pallas as pl
from jax.experimental.pallas import tpu as pltpu
from jax.sharding import PartitionSpec as P

LANES = 256
F32 = jnp.float32
BF16 = jnp.bfloat16
MESH = pl.DeviceIdType.MESH
STATE_SUB = 4
MAIN_SUB = 2


def split(value):
    high = value.astype(BF16)
    return high, (value - high.astype(F32)).astype(BF16)


def mul(a, b):
    return jnp.dot(a, b, preferred_element_type=F32)


def twice(value, axis):
    return jnp.concatenate([value, value], axis=axis)


def exact_right(left, right):
    return mul(jnp.concatenate(split(left), axis=1), right)


def three(left, right):
    left_high, left_low = split(left)
    right_high, right_low = split(right)
    return mul(left_high, right_high) + (mul(left_low, right_high) + mul(left_high, right_low))


def own_rows(wide, modes, group):
    rows, lanes = wide.shape
    owner = lax.broadcasted_iota(jnp.int32, (modes, lanes), 1) // group
    out = wide[:modes]
    for g in range(1, rows // modes):
        out = jnp.where(owner == g, wide[g * modes : (g + 1) * modes], out)
    return out


def spread(narrow, rows, group):
    modes, lanes = narrow.shape
    owner = lax.broadcasted_iota(jnp.int32, (modes, lanes), 1) // group
    return jnp.concatenate(
        [jnp.where(owner == g, narrow, 0.0) for g in range(rows // modes)], axis=0
    )


def states_kernel(modes, group, rate_ref, x_ref, g_ref, state_ref, weighted_ref):
    length = x_ref.shape[0]
    for j in range(rate_ref.shape[0]):
        lanes = slice(j * LANES, (j + 1) * LANES)
        rate = rate_ref[j]
        at = lax.broadcasted_iota(jnp.int32, (length, rate.shape[1]), 0).astype(F32)
        rising = jnp.exp(-rate * at)
        falling = jnp.exp(-rate * (length - 1.0 - at))
        for k, (table, weight, values) in enumerate(
            ((falling, length - at, x_ref[:, lanes]), (rising, at, g_ref[:, lanes]))
        ):
            left = jnp.concatenate([table.T, (weight * table).T], axis=0)
            both = exact_right(left, twice(values, 0))
            rows = table.shape[1]
            state_ref[k, :, lanes] = own_rows(both[:rows], modes, group)
            weighted_ref[k, :, lanes] = own_rows(both[rows:], modes, group)


def main_kernel(
    modes, group, rate_ref, pole_ref, gap_ref, dft_ref, inv_high_ref, inv_low_ref, angle_ref,
    x_ref, g_ref, res_ref, rates_ref, state_ref, weighted_ref, carry_ref,
    y_ref, gs_ref, gres_ref, grate_ref,
):
    sub = rate_ref.shape[0]
    for j in range(sub):
        lanes = slice(j * LANES, (j + 1) * LANES)
        main_block(
            modes, group, j, rate_ref, pole_ref, gap_ref, dft_ref, inv_high_ref, inv_low_ref, angle_ref,
            x_ref.at[:, lanes], g_ref.at[:, lanes], res_ref.at[:, lanes], rates_ref.at[:, lanes],
            state_ref.at[:, :, lanes], weighted_ref.at[:, :, lanes], carry_ref.at[:, :, lanes],
            y_ref.at[:, lanes], gs_ref.at[:, lanes], gres_ref.at[:, lanes], grate_ref,
        )


def main_block(
    modes, group, j, rate_ref, pole_ref, gap_ref, dft_ref, inv_high_ref, inv_low_ref, angle_ref,
    x_ref, g_ref, res_ref, rates_ref, state_ref, weighted_ref, carry_ref,
    y_ref, gs_ref, gres_ref, grate_ref,
):
    length = x_ref.shape[0]
    half = length // 2
    rate = rate_ref[j]
    pole = pole_ref[j]
    gap = gap_ref[j]
    gm = rate.shape[1]
    scale = 1.0 / half
    real = gap + pole * angle_ref[0]
    imag = pole * angle_ref[1]
    inverse = 1.0 / (real * real + imag * imag)
    phi_r = real * inverse
    phi_i = -imag * inverse
    psi_r = phi_r * phi_r - phi_i * phi_i - phi_r
    psi_i = 2.0 * phi_r * phi_i - phi_i
    phi = jnp.concatenate([phi_r, phi_i], axis=0)
    phi_t = jnp.concatenate([phi_r, -phi_i], axis=0).T
    psi_t = jnp.concatenate([psi_r, -psi_i], axis=0).T
    x_hat = mul(dft_ref[...], twice(x_ref[...], 0))
    g_hat = mul(dft_ref[...], twice(g_ref[...], 0))
    res = res_ref[...]
    phi_high, phi_low = split(phi)
    res_wide = spread(res, gm, group)
    res_high, res_low = split(res_wide)
    k_hat = mul(jnp.concatenate([phi_high, phi_low], 1), twice(res_high, 0)) + mul(phi_high, res_low)
    xr, xi = x_hat[:half], x_hat[half:]
    gr, gi = g_hat[:half], g_hat[half:]
    kr, ki = k_hat[:half], k_hat[half:]
    y_hat = jnp.concatenate([kr * xr - ki * xi, kr * xi + ki * xr], axis=0)
    h_hat = jnp.concatenate([kr * gr + ki * gi, kr * gi - ki * gr], axis=0)
    lag = jnp.concatenate([gr * xr + gi * xi, gr * xi - gi * xr], axis=0) * scale
    lane_rate = rates_ref[...]
    lane_pole = jnp.exp(-lane_rate)
    whole = jnp.exp(-lane_rate * length)
    fold = 1.0 / (1.0 + whole)
    s_x, s_g = state_ref[0], state_ref[1]
    carry, adjoint = carry_ref[0], carry_ref[1]
    turned_x, turned_g = s_x * fold, s_g * fold
    carry_all = carry + turned_x
    adjoint_all = adjoint + turned_g
    at = lax.broadcasted_iota(jnp.int32, (length, gm), 0).astype(F32)
    rising = jnp.exp(-rate * (at + 1.0))
    falling = jnp.exp(-rate * (length - at))
    for table, hat, start, out in (
        (rising, y_hat, carry_all, y_ref),
        (falling, h_hat, adjoint_all, gs_ref),
    ):
        table_high, table_low = split(table)
        left_high = jnp.concatenate([inv_high_ref[...], table_high], axis=1)
        left_low = jnp.concatenate([inv_low_ref[...], table_low], axis=1)
        right = jnp.concatenate([hat, spread(res * start, gm, group)], axis=0)
        right_high, right_low = split(right)
        total = mul(left_high, right_high) + mul(left_low, right_high) + mul(left_high, right_low)
        out[...] = total.astype(BF16)
    terms = jnp.concatenate([phi_t, psi_t], axis=0)
    terms_high, terms_low = split(terms)
    lag_high, lag_low = split(lag)
    wide = mul(jnp.concatenate([terms_high, terms_low], 1), twice(lag_high, 0)) + mul(
        terms_high, lag_low
    )
    sums = own_rows(wide[:gm], modes, group) + carry_all * lane_pole * s_g
    moments = (
        own_rows(wide[gm:], modes, group)
        + lane_pole * (carry_all * weighted_ref[1] + adjoint_all * weighted_ref[0])
        + length * lane_pole * whole * (carry * adjoint - turned_x * turned_g)
    )
    gres_ref[...] = sums
    rm = -lane_rate * res * moments
    sub = rate_ref.shape[0]
    per = LANES // group
    step = lax.rem(pl.program_id(0) * sub + j, 128 // per)
    rows = lax.broadcasted_iota(jnp.int32, (LANES, 128), 0) // group
    cols = lax.broadcasted_iota(jnp.int32, (LANES, 128), 1)
    pick = jnp.where(rows + step * per == cols, 1.0, 0.0).astype(BF16)
    both = mul(jnp.concatenate(split(rm), 0), pick)
    added = both[:modes] + both[modes:]
    if j == 0:
        @pl.when(step == 0)
        def _():
            grate_ref[...] = jnp.zeros_like(grate_ref)
    grate_ref[...] += added


def barrier_with(peers):
    barrier = pltpu.get_barrier_semaphore()
    for axis, peer in peers:
        pl.semaphore_signal(barrier, inc=1, device_id={axis: peer}, device_id_type=MESH)
    pl.semaphore_wait(barrier, len(peers))


def send(source, target, send_sem, recv_sem, axis, peer):
    copy = pltpu.make_async_remote_copy(
        src_ref=source, dst_ref=target, send_sem=send_sem, recv_sem=recv_sem,
        device_id={axis: peer}, device_id_type=MESH,
    )
    copy.start()
    return copy


def carry_kernel(
    n, length, state_ref, rate_ref, out_ref, inbox, outbox, landed, send_a, recv_a, send_b, recv_b
):
    me = lax.axis_index("seq")
    width = state_ref.shape[2] // n
    others = [lax.rem(me + k, n) for k in range(1, n)]

    def lanes(index):
        return pl.ds(pl.multiple_of(index * width, 128), width)

    barrier_with([("seq", peer) for peer in others])
    first = [
        send(state_ref.at[:, :, lanes(peer)], inbox.at[me], send_a.at[k], recv_a.at[k], "seq", peer)
        for k, peer in enumerate(others)
    ]
    inbox[me] = state_ref[:, :, lanes(me)]
    whole = jnp.exp(-rate_ref[:, lanes(me)] * length)
    for copy in first:
        copy.wait_recv()
    carry = jnp.zeros_like(whole)
    adjoint = jnp.zeros_like(whole)
    for i in range(n):
        outbox[i, 0] = carry
        carry = inbox[i, 0] + whole * carry
        last = n - 1 - i
        outbox[last, 1] = adjoint
        adjoint = inbox[last, 1] + whole * adjoint
    second = [
        send(outbox.at[peer], landed.at[:, :, lanes(me)], send_b.at[k], recv_b.at[k], "seq", peer)
        for k, peer in enumerate(others)
    ]
    landed[:, :, lanes(me)] = outbox[me]
    for copy in second:
        copy.wait_recv()
    out_ref[...] = landed[...]
    for copy in first + second:
        copy.wait_send()


def reduce_kernel(
    n, rows, norm, res_ref, rate_ref, res_out, rate_out, inbox, inrate, rowbox, rowrate, landed,
    send_a, recv_a, send_b, recv_b, send_c, recv_c, send_d, recv_d, send_e, recv_e,
):
    me = lax.axis_index("seq")
    mine = lax.axis_index("batch")
    width = res_ref.shape[1] // n
    others = [lax.rem(me + k, n) for k in range(1, n)]
    beside = [lax.rem(mine + k, rows) for k in range(1, rows)]

    def lanes(index):
        return pl.ds(pl.multiple_of(index * width, 128), width)

    barrier_with([("seq", peer) for peer in others] + [("batch", peer) for peer in beside])
    copies = []
    for k, peer in enumerate(others):
        copies += [
            send(res_ref.at[:, lanes(peer)], inbox.at[me], send_a.at[k], recv_a.at[k], "seq", peer),
            send(rate_ref, inrate.at[me], send_b.at[k], recv_b.at[k], "seq", peer),
        ]
    inbox[me] = res_ref[:, lanes(me)]
    inrate[me] = rate_ref[...]
    for copy in copies:
        copy.wait_recv()
    part, rate_part = inbox[0], inrate[0]
    for i in range(1, n):
        part = part + inbox[i]
        rate_part = rate_part + inrate[i]
    rowbox[mine] = part
    rowrate[mine] = rate_part
    across = []
    for k, peer in enumerate(beside):
        across += [
            send(rowbox.at[mine], rowbox.at[mine], send_c.at[k], recv_c.at[k], "batch", peer),
            send(rowrate.at[mine], rowrate.at[mine], send_d.at[k], recv_d.at[k], "batch", peer),
        ]
    for copy in across:
        copy.wait_recv()
    part, rate_part = rowbox[0], rowrate[0]
    for i in range(1, rows):
        part = part + rowbox[i]
        rate_part = rate_part + rowrate[i]
    landed[:, lanes(me)] = part * norm
    back = [
        send(landed.at[:, lanes(me)], landed.at[:, lanes(me)], send_e.at[k], recv_e.at[k], "seq", peer)
        for k, peer in enumerate(others)
    ]
    rate_out[...] = rate_part * norm
    for copy in back:
        copy.wait_recv()
    res_out[...] = landed[...]
    for copy in copies + across + back:
        copy.wait_send()


def constants(length):
    half = length // 2
    omega = np.pi * (2.0 * np.arange(half) + 1.0) / length
    at = np.arange(length)
    forward = np.concatenate([np.cos(np.outer(omega, at)), -np.sin(np.outer(omega, at))], axis=0)
    lanes = np.ones((1, 128))
    angle = np.stack(
        [2.0 * np.sin(omega / 2.0)[:, None] ** 2 * lanes, np.sin(omega)[:, None] * lanes]
    )
    return forward.astype(np.float32), (forward.T / half).astype(np.float32), angle.astype(np.float32)


def local(mesh_shape, signal, out_grad, residues, log_rates):
    batch_rows, length, channels = signal.shape
    modes, groups = log_rates.shape
    group = channels // groups
    blocks = channels // LANES
    gm = LANES // group * modes
    norm = 1.0 / (batch_rows * mesh_shape["batch"] * length * mesh_shape["seq"])
    decay = jnp.exp(log_rates)
    flat = decay.T.reshape(blocks, 1, gm)
    pole = jnp.exp(-flat)
    gap = -jnp.expm1(-flat)
    lane_rate = jnp.repeat(decay, group, axis=1)
    forward, inverse, angle = constants(length)
    dft_high = jnp.asarray(forward).astype(BF16)
    dft = jnp.concatenate(
        [dft_high, (jnp.asarray(forward) - dft_high.astype(F32)).astype(BF16)], axis=1
    )
    inv_high, inv_low = split(jnp.asarray(inverse))
    angle = jnp.asarray(angle)
    peers, rows = mesh_shape["seq"], mesh_shape["batch"]
    width = channels // peers
    lane_pick = 128 // (LANES // group)

    def specs(sub):
        return (
            pl.BlockSpec((sub, 1, gm), lambda b: (b, 0, 0)),
            pl.BlockSpec((length, sub * LANES), lambda b: (0, b)),
            pl.BlockSpec((modes, sub * LANES), lambda b: (0, b)),
            pl.BlockSpec((2, modes, sub * LANES), lambda b: (0, 0, b)),
        )

    def fixed(shape):
        return pl.BlockSpec(shape, lambda b: (0,) * len(shape))

    def dma(count):
        return pltpu.SemaphoreType.DMA((max(count, 1),))

    vmem = pl.BlockSpec(memory_space=pltpu.VMEM)
    pair = jax.ShapeDtypeStruct((2, modes, channels), F32)
    mixed, grads, res_sum, rate_sum = [], [], 0.0, 0.0
    for row in range(batch_rows):
        x, g = signal[row], out_grad[row]
        row_spec, data_spec, lane_spec, pair_spec = specs(STATE_SUB)
        state, weighted = pl.pallas_call(
            functools.partial(states_kernel, modes, group),
            grid=(blocks // STATE_SUB,),
            in_specs=[row_spec, data_spec, data_spec],
            out_specs=[pair_spec, pair_spec],
            out_shape=[pair, pair],
        )(flat, x, g)
        carry = pl.pallas_call(
            functools.partial(carry_kernel, peers, float(length)),
            in_specs=[vmem, vmem],
            out_specs=vmem,
            out_shape=pair,
            scratch_shapes=[
                pltpu.VMEM((peers, 2, modes, width), F32),
                pltpu.VMEM((peers, 2, modes, width), F32),
                pltpu.VMEM((2, modes, channels), F32),
            ]
            + [dma(peers - 1)] * 4,
            compiler_params=pltpu.CompilerParams(collective_id=0, has_side_effects=True),
        )(state, lane_rate)
        row_spec, data_spec, lane_spec, pair_spec = specs(MAIN_SUB)
        y, gs, part, rates = pl.pallas_call(
            functools.partial(main_kernel, modes, group),
            grid=(blocks // MAIN_SUB,),
            in_specs=[
                row_spec, row_spec, row_spec,
                fixed(dft.shape), fixed(inv_high.shape), fixed(inv_low.shape), fixed(angle.shape),
                data_spec, data_spec, lane_spec, lane_spec, pair_spec, pair_spec, pair_spec,
            ],
            out_specs=[
                data_spec, data_spec, lane_spec,
                pl.BlockSpec((modes, 128), lambda b: (0, b * MAIN_SUB // lane_pick)),
            ],
            out_shape=[
                jax.ShapeDtypeStruct((length, channels), BF16),
                jax.ShapeDtypeStruct((length, channels), BF16),
                jax.ShapeDtypeStruct((modes, channels), F32),
                jax.ShapeDtypeStruct((modes, groups), F32),
            ],
        )(flat, pole, gap, dft, inv_high, inv_low, angle, x, g, residues, lane_rate, state, weighted, carry)
        mixed.append(y)
        grads.append(gs)
        res_sum = res_sum + part if row else part
        rate_sum = rate_sum + rates if row else rates
    res_sum, rate_sum = pl.pallas_call(
        functools.partial(reduce_kernel, peers, rows, norm),
        in_specs=[vmem, vmem],
        out_specs=[vmem, vmem],
        out_shape=[
            jax.ShapeDtypeStruct((modes, channels), F32),
            jax.ShapeDtypeStruct((modes, groups), F32),
        ],
        scratch_shapes=[
            pltpu.VMEM((peers, modes, width), F32),
            pltpu.VMEM((peers, modes, groups), F32),
            pltpu.VMEM((rows, modes, width), F32),
            pltpu.VMEM((rows, modes, groups), F32),
            pltpu.VMEM((modes, channels), F32),
        ]
        + [dma(peers - 1)] * 4 + [dma(rows - 1)] * 4 + [dma(peers - 1)] * 2,
        compiler_params=pltpu.CompilerParams(collective_id=1, has_side_effects=True),
    )(res_sum, rate_sum)
    return jnp.stack(mixed), jnp.stack(grads), res_sum, rate_sum


def solution(mesh):
    placed = (P("batch", "seq", None), P("batch", "seq", None), P(), P())
    return jax.shard_map(
        functools.partial(local, dict(mesh.shape)),
        mesh=mesh,
        in_specs=placed,
        out_specs=placed,
        check_vma=False,
    )
```

```python
import functools

import jax
import jax.numpy as jnp
import numpy as np
from jax import lax
from jax.experimental import pallas as pl
from jax.experimental.pallas import tpu as pltpu
from jax.sharding import PartitionSpec as P

LANES = 256
F32 = jnp.float32
BF16 = jnp.bfloat16
MESH = pl.DeviceIdType.MESH
STATE_SUB = 4
MAIN_SUB = 2


def split(value):
    high = value.astype(BF16)
    return high, (value - high.astype(F32)).astype(BF16)


def mul(a, b):
    return jnp.dot(a, b, preferred_element_type=F32)


def twice(value, axis):
    return jnp.concatenate([value, value], axis=axis)


def exact_right(left, right):
    return mul(jnp.concatenate(split(left), axis=1), right)


def own_rows(wide, modes, group):
    rows, lanes = wide.shape
    owner = lax.broadcasted_iota(jnp.int32, (modes, lanes), 1) // group
    out = wide[:modes]
    for g in range(1, rows // modes):
        out = jnp.where(owner == g, wide[g * modes : (g + 1) * modes], out)
    return out


def spread(narrow, rows, group):
    modes, lanes = narrow.shape
    owner = lax.broadcasted_iota(jnp.int32, (modes, lanes), 1) // group
    return jnp.concatenate(
        [jnp.where(owner == g, narrow, 0.0) for g in range(rows // modes)], axis=0
    )


def states_kernel(modes, group, rate_ref, x_ref, g_ref, state_ref, weighted_ref):
    length = x_ref.shape[0]
    for j in range(rate_ref.shape[0]):
        lanes = slice(j * LANES, (j + 1) * LANES)
        rate = rate_ref[j]
        at = lax.broadcasted_iota(jnp.int32, (length, rate.shape[1]), 0).astype(F32)
        rising = jnp.exp(-rate * at)
        falling = jnp.exp(-rate * (length - 1.0 - at))
        for k, (table, weight, values) in enumerate(
            ((falling, length - at, x_ref[:, lanes]), (rising, at, g_ref[:, lanes]))
        ):
            left = jnp.concatenate([table.T, (weight * table).T], axis=0)
            both = exact_right(left, twice(values, 0))
            rows = table.shape[1]
            state_ref[k, :, lanes] = own_rows(both[:rows], modes, group)
            weighted_ref[k, :, lanes] = own_rows(both[rows:], modes, group)


def nega_block(
    modes, group, pole, gap, dft, inv_high, inv_low, angle, x, g, res,
):
    half = x.shape[0] // 2
    gm = pole.shape[1]
    real = gap + pole * angle[0]
    imag = pole * angle[1]
    inverse = 1.0 / (real * real + imag * imag)
    phi_r = real * inverse
    phi_i = -imag * inverse
    psi_r = phi_r * phi_r - phi_i * phi_i - phi_r
    psi_i = 2.0 * phi_r * phi_i - phi_i
    phi = jnp.concatenate([phi_r, phi_i], axis=0)
    phi_t = jnp.concatenate([phi_r, -phi_i], axis=0).T
    psi_t = jnp.concatenate([psi_r, -psi_i], axis=0).T
    x_hat = mul(dft, twice(x, 0))
    g_hat = mul(dft, twice(g, 0))
    phi_high, phi_low = split(phi)
    res_high, res_low = split(spread(res, gm, group))
    k_hat = mul(jnp.concatenate([phi_high, phi_low], 1), twice(res_high, 0)) + mul(phi_high, res_low)
    xr, xi = x_hat[:half], x_hat[half:]
    gr, gi = g_hat[:half], g_hat[half:]
    kr, ki = k_hat[:half], k_hat[half:]
    y_hat = jnp.concatenate([kr * xr - ki * xi, kr * xi + ki * xr], axis=0)
    h_hat = jnp.concatenate([kr * gr + ki * gi, kr * gi - ki * gr], axis=0)
    lag = jnp.concatenate([gr * xr + gi * xi, gr * xi - gi * xr], axis=0) * (1.0 / half)
    inv_both = jnp.concatenate([inv_high, inv_low], axis=1)
    outs = []
    for hat in (y_hat, h_hat):
        hat_high, hat_low = split(hat)
        outs.append(mul(inv_both, twice(hat_high, 0)) + mul(inv_high, hat_low))
    terms_high, terms_low = split(jnp.concatenate([phi_t, psi_t], axis=0))
    lag_high, lag_low = split(lag)
    wide = mul(jnp.concatenate([terms_high, terms_low], 1), twice(lag_high, 0)) + mul(
        terms_high, lag_low
    )
    return outs + [own_rows(wide[:gm], modes, group), own_rows(wide[gm:], modes, group)]


def carry_block(group, table, start):
    high, low = split(table)
    start_high, start_low = split(spread(start, table.shape[1], group))
    return mul(jnp.concatenate([high, low], 1), twice(start_high, 0)) + mul(high, start_low)


def remote(source, target, sems, k, axis, peer):
    return pltpu.make_async_remote_copy(
        src_ref=source, dst_ref=target, send_sem=sems[0].at[k], recv_sem=sems[1].at[k],
        device_id={axis: peer}, device_id_type=MESH,
    )


def whole_kernel(
    n, rows, norm, modes, group, steps,
    rate_ref, pole_ref, gap_ref, dft_ref, inv_high_ref, inv_low_ref, angle_ref, x_ref, g_ref,
    res_ref, rates_ref, state_ref, weighted_ref,
    y_ref, gs_ref, gres_ref, grate_ref,
    inbox, outbox, landed, y_held, gs_held, sum_held, moment_held, rate_held,
    sumbox, ratebox, rowbox, rowrate, gathered, *sems,
):
    step = pl.program_id(0)
    sub = rate_ref.shape[0]
    length = x_ref.shape[0]
    channels = res_ref.shape[1]
    span = sub * LANES
    me = lax.axis_index("seq")
    mine = lax.axis_index("batch")
    width = channels // n
    others = [lax.rem(me + k, n) for k in range(1, n)]
    beside = [lax.rem(mine + k, rows) for k in range(1, rows)]
    pairs = [(sems[2 * i], sems[2 * i + 1]) for i in range(7)]

    def lanes(index):
        return pl.ds(pl.multiple_of(index * width, 128), width)

    def first():
        return [
            remote(state_ref.at[:, :, lanes(p)], inbox.at[me], pairs[0], k, "seq", p)
            for k, p in enumerate(others)
        ]

    def second():
        return [
            remote(outbox.at[p], landed.at[:, :, lanes(me)], pairs[1], k, "seq", p)
            for k, p in enumerate(others)
        ]

    def third():
        return [
            remote(sum_held.at[:, lanes(p)], sumbox.at[me], pairs[2], k, "seq", p)
            for k, p in enumerate(others)
        ] + [
            remote(rate_held, ratebox.at[me], pairs[3], k, "seq", p) for k, p in enumerate(others)
        ]

    def fourth():
        return [
            remote(rowbox.at[mine], rowbox.at[mine], pairs[4], k, "batch", p)
            for k, p in enumerate(beside)
        ] + [
            remote(rowrate.at[mine], rowrate.at[mine], pairs[5], k, "batch", p)
            for k, p in enumerate(beside)
        ]

    def fifth():
        return [
            remote(gathered.at[:, lanes(me)], gathered.at[:, lanes(me)], pairs[6], k, "seq", p)
            for k, p in enumerate(others)
        ]

    @pl.when(step == 0)
    def _():
        barrier = pltpu.get_barrier_semaphore()
        for p in others:
            pl.semaphore_signal(barrier, inc=1, device_id={"seq": p}, device_id_type=MESH)
        for p in beside:
            pl.semaphore_signal(barrier, inc=1, device_id={"batch": p}, device_id_type=MESH)
        pl.semaphore_wait(barrier, len(others) + len(beside))
        for copy in first():
            copy.start()

    @pl.when(step == steps // 2)
    def _():
        for copy in first():
            copy.wait_recv()
        inbox[me] = state_ref[:, :, lanes(me)]
        whole = jnp.exp(-rates_ref[:, lanes(me)] * float(length))
        carry = jnp.zeros_like(whole)
        adjoint = jnp.zeros_like(whole)
        for i in range(n):
            outbox[i, 0] = carry
            carry = inbox[i, 0] + whole * carry
            last = n - 1 - i
            outbox[last, 1] = adjoint
            adjoint = inbox[last, 1] + whole * adjoint
        for copy in second():
            copy.start()
        landed[:, :, lanes(me)] = outbox[me]

    @pl.when(step < steps)
    def _():
        for j in range(sub):
            here = slice(j * LANES, (j + 1) * LANES)
            at = pl.ds(pl.multiple_of(step * span + j * LANES, 128), LANES)
            y, gs, sums, moments = nega_block(
                modes, group, pole_ref[j], gap_ref[j], dft_ref[...], inv_high_ref[...],
                inv_low_ref[...], angle_ref[...], x_ref[:, here], g_ref[:, here], res_ref[:, at],
            )
            y_held[:, at] = y
            gs_held[:, at] = gs
            sum_held[:, at] = sums
            moment_held[:, at] = moments

    @pl.when(step == steps)
    def _():
        for copy in second():
            copy.wait_recv()
        per = LANES // group
        many = 128 // per
        row_id = lax.broadcasted_iota(jnp.int32, (LANES, 128), 0) // group
        col_id = lax.broadcasted_iota(jnp.int32, (LANES, 128), 1)

        def lap(c, nothing):
            added = jnp.zeros((2 * modes, 128), F32)
            for j in range(many):
                at = pl.ds(pl.multiple_of((c * many + j) * LANES, 128), LANES)
                rate = rates_ref[:, at]
                pole = jnp.exp(-rate)
                whole = jnp.exp(-rate * float(length))
                fold = 1.0 / (1.0 + whole)
                s_x, s_g = state_ref[0, :, at], state_ref[1, :, at]
                carry, adjoint = landed[0, :, at], landed[1, :, at]
                turned_x, turned_g = s_x * fold, s_g * fold
                carry_all, adjoint_all = carry + turned_x, adjoint + turned_g
                res = res_ref[:, at]
                sum_held[:, at] = sum_held[:, at] + carry_all * pole * s_g
                moments = (
                    moment_held[:, at]
                    + pole * (carry_all * weighted_ref[1, :, at] + adjoint_all * weighted_ref[0, :, at])
                    + float(length) * pole * whole * (carry * adjoint - turned_x * turned_g)
                )
                landed[0, :, at] = res * carry_all
                landed[1, :, at] = res * adjoint_all
                pick = jnp.where(row_id + j * per == col_id, 1.0, 0.0).astype(BF16)
                added += mul(jnp.concatenate(split(-rate * res * moments), 0), pick)
            rate_held[:, pl.ds(pl.multiple_of(c * 128, 128), 128)] = added[:modes] + added[modes:]
            return nothing

        lax.fori_loop(0, channels // (LANES * many), lap, 0)
        for copy in third():
            copy.start()
        sumbox[me] = sum_held[:, lanes(me)]
        ratebox[me] = rate_held[...]

    @pl.when(step >= steps)
    def _():
        for j in range(sub):
            here = slice(j * LANES, (j + 1) * LANES)
            at = pl.ds(pl.multiple_of((step - steps) * span + j * LANES, 128), LANES)
            rate = rate_ref[j]
            when = lax.broadcasted_iota(jnp.int32, (length, rate.shape[1]), 0).astype(F32)
            rising = jnp.exp(-rate * (when + 1.0))
            falling = jnp.exp(-rate * (length - when))
            y = y_held[:, at] + carry_block(group, rising, landed[0, :, at])
            y_ref[:, here] = y.astype(BF16)
            gs = gs_held[:, at] + carry_block(group, falling, landed[1, :, at])
            gs_ref[:, here] = gs.astype(BF16)

    @pl.when(step == 2 * steps - 1)
    def _():
        for copy in third():
            copy.wait_recv()
        part, rate_part = sumbox[0], ratebox[0]
        for i in range(1, n):
            part = part + sumbox[i]
            rate_part = rate_part + ratebox[i]
        rowbox[mine] = part
        rowrate[mine] = rate_part
        for copy in fourth():
            copy.start()
        for copy in fourth():
            copy.wait_recv()
        part, rate_part = rowbox[0], rowrate[0]
        for i in range(1, rows):
            part = part + rowbox[i]
            rate_part = rate_part + rowrate[i]
        gathered[:, lanes(me)] = part * norm
        for copy in fifth():
            copy.start()
        grate_ref[...] = rate_part * norm
        for copy in fifth():
            copy.wait_recv()
        gres_ref[...] = gathered[...]
        for copy in first() + second() + third() + fourth() + fifth():
            copy.wait_send()


def constants(length):
    half = length // 2
    omega = np.pi * (2.0 * np.arange(half) + 1.0) / length
    at = np.arange(length)
    forward = np.concatenate([np.cos(np.outer(omega, at)), -np.sin(np.outer(omega, at))], axis=0)
    lanes = np.ones((1, 128))
    angle = np.stack(
        [2.0 * np.sin(omega / 2.0)[:, None] ** 2 * lanes, np.sin(omega)[:, None] * lanes]
    )
    return forward.astype(np.float32), (forward.T / half).astype(np.float32), angle.astype(np.float32)


def local(mesh_shape, signal, out_grad, residues, log_rates):
    batch_rows, length, channels = signal.shape
    modes, groups = log_rates.shape
    group = channels // groups
    blocks = channels // LANES
    gm = LANES // group * modes
    norm = 1.0 / (batch_rows * mesh_shape["batch"] * length * mesh_shape["seq"])
    decay = jnp.exp(log_rates)
    flat = decay.T.reshape(blocks, 1, gm)
    pole = jnp.exp(-flat)
    gap = -jnp.expm1(-flat)
    lane_rate = jnp.repeat(decay, group, axis=1)
    forward, inverse, angle = constants(length)
    dft_high = jnp.asarray(forward).astype(BF16)
    dft = jnp.concatenate(
        [dft_high, (jnp.asarray(forward) - dft_high.astype(F32)).astype(BF16)], axis=1
    )
    inv_high, inv_low = split(jnp.asarray(inverse))
    angle = jnp.asarray(angle)
    peers, rows = mesh_shape["seq"], mesh_shape["batch"]
    width = channels // peers

    def specs(sub):
        return (
            pl.BlockSpec((sub, 1, gm), lambda b: (b, 0, 0)),
            pl.BlockSpec((length, sub * LANES), lambda b: (0, b)),
            pl.BlockSpec((modes, sub * LANES), lambda b: (0, b)),
            pl.BlockSpec((2, modes, sub * LANES), lambda b: (0, 0, b)),
        )

    def fixed(shape):
        return pl.BlockSpec(shape, lambda b: (0,) * len(shape))

    def dma(count):
        return pltpu.SemaphoreType.DMA((max(count, 1),))

    pair = jax.ShapeDtypeStruct((2, modes, channels), F32)
    mixed, grads, res_sum, rate_sum = [], [], 0.0, 0.0
    for row in range(batch_rows):
        x, g = signal[row], out_grad[row]
        row_spec, data_spec, lane_spec, pair_spec = specs(STATE_SUB)
        state, weighted = pl.pallas_call(
            functools.partial(states_kernel, modes, group),
            grid=(blocks // STATE_SUB,),
            in_specs=[row_spec, data_spec, data_spec],
            out_specs=[pair_spec, pair_spec],
            out_shape=[pair, pair],
        )(flat, x, g)
        steps = blocks // MAIN_SUB
        wide = MAIN_SUB * LANES
        y, gs, part, rates = pl.pallas_call(
            functools.partial(whole_kernel, peers, rows, norm, modes, group, steps),
            grid=(2 * steps,),
            in_specs=[pl.BlockSpec((MAIN_SUB, 1, gm), lambda b: (b % steps, 0, 0))] * 3
            + [fixed(v.shape) for v in (dft, inv_high, inv_low, angle)]
            + [pl.BlockSpec((length, wide), lambda b: (0, jnp.minimum(b, steps - 1)))] * 2
            + [fixed(residues.shape), fixed(lane_rate.shape), fixed(pair.shape), fixed(pair.shape)],
            out_specs=[pl.BlockSpec((length, wide), lambda b: (0, jnp.maximum(b - steps, 0)))] * 2
            + [fixed((modes, channels)), fixed((modes, groups))],
            out_shape=[
                jax.ShapeDtypeStruct((length, channels), BF16),
                jax.ShapeDtypeStruct((length, channels), BF16),
                jax.ShapeDtypeStruct((modes, channels), F32),
                jax.ShapeDtypeStruct((modes, groups), F32),
            ],
            scratch_shapes=[
                pltpu.VMEM((peers, 2, modes, width), F32),
                pltpu.VMEM((peers, 2, modes, width), F32),
                pltpu.VMEM((2, modes, channels), F32),
                pltpu.VMEM((length, channels), F32),
                pltpu.VMEM((length, channels), F32),
                pltpu.VMEM((modes, channels), F32),
                pltpu.VMEM((modes, channels), F32),
                pltpu.VMEM((modes, groups), F32),
                pltpu.VMEM((peers, modes, width), F32),
                pltpu.VMEM((peers, modes, groups), F32),
                pltpu.VMEM((rows, modes, width), F32),
                pltpu.VMEM((rows, modes, groups), F32),
                pltpu.VMEM((modes, channels), F32),
            ]
            + [dma(peers - 1)] * 8 + [dma(rows - 1)] * 4 + [dma(peers - 1)] * 2,
            compiler_params=pltpu.CompilerParams(collective_id=0, has_side_effects=True),
        )(flat, pole, gap, dft, inv_high, inv_low, angle, x, g, residues, lane_rate, state, weighted)
        mixed.append(y)
        grads.append(gs)
        res_sum = res_sum + part if row else part
        rate_sum = rate_sum + rates if row else rates
    return jnp.stack(mixed), jnp.stack(grads), res_sum, rate_sum


def solution(mesh):
    placed = (P("batch", "seq", None), P("batch", "seq", None), P(), P())
    return jax.shard_map(
        functools.partial(local, dict(mesh.shape)),
        mesh=mesh,
        in_specs=placed,
        out_specs=placed,
        check_vma=False,
    )
```

```python
import functools

import jax
import jax.numpy as jnp
import numpy as np
from jax import lax
from jax.experimental import pallas as pl
from jax.experimental.pallas import tpu as pltpu
from jax.sharding import PartitionSpec as P

LANES = 256
F32 = jnp.float32
BF16 = jnp.bfloat16
MESH = pl.DeviceIdType.MESH
STATE_SUB = 4
MAIN_SUB = 4


def split(value):
    high = value.astype(BF16)
    return high, (value - high.astype(F32)).astype(BF16)


def mul(a, b):
    return jnp.dot(a, b, preferred_element_type=F32)


def twice(value, axis):
    return jnp.concatenate([value, value], axis=axis)


def exact_right(left, right):
    return mul(jnp.concatenate(split(left), axis=1), right)


def own_rows(wide, modes, group):
    rows, lanes = wide.shape
    owner = lax.broadcasted_iota(jnp.int32, (modes, lanes), 1) // group
    out = wide[:modes]
    for g in range(1, rows // modes):
        out = jnp.where(owner == g, wide[g * modes : (g + 1) * modes], out)
    return out


def spread(narrow, rows, group):
    modes, lanes = narrow.shape
    owner = lax.broadcasted_iota(jnp.int32, (modes, lanes), 1) // group
    return jnp.concatenate(
        [jnp.where(owner == g, narrow, 0.0) for g in range(rows // modes)], axis=0
    )


def states_kernel(modes, group, rate_ref, x_ref, g_ref, state_ref, weighted_ref):
    length = x_ref.shape[0]
    for j in range(rate_ref.shape[0]):
        lanes = slice(j * LANES, (j + 1) * LANES)
        rate = rate_ref[j]
        at = lax.broadcasted_iota(jnp.int32, (length, rate.shape[1]), 0).astype(F32)
        rising = jnp.exp(-rate * at)
        falling = jnp.exp(-rate * (length - 1.0 - at))
        for k, (table, weight, values) in enumerate(
            ((falling, length - at, x_ref[:, lanes]), (rising, at, g_ref[:, lanes]))
        ):
            left = jnp.concatenate([table.T, (weight * table).T], axis=0)
            both = exact_right(left, twice(values, 0))
            rows = table.shape[1]
            state_ref[k, :, lanes] = own_rows(both[:rows], modes, group)
            weighted_ref[k, :, lanes] = own_rows(both[rows:], modes, group)


def nega_block(
    modes, group, pole, gap, dft, inv_high, inv_low, angle, x, g, res,
):
    half = x.shape[0] // 2
    gm = pole.shape[1]
    real = gap + pole * angle[0]
    imag = pole * angle[1]
    inverse = 1.0 / (real * real + imag * imag)
    phi_r = real * inverse
    phi_i = -imag * inverse
    psi_r = phi_r * phi_r - phi_i * phi_i - phi_r
    psi_i = 2.0 * phi_r * phi_i - phi_i
    phi = jnp.concatenate([phi_r, phi_i], axis=0)
    phi_t = jnp.concatenate([phi_r, -phi_i], axis=0).T
    psi_t = jnp.concatenate([psi_r, -psi_i], axis=0).T
    x_hat = mul(dft, twice(x, 0))
    g_hat = mul(dft, twice(g, 0))
    phi_high, phi_low = split(phi)
    res_high, res_low = split(spread(res, gm, group))
    k_hat = mul(jnp.concatenate([phi_high, phi_low], 1), twice(res_high, 0)) + mul(phi_high, res_low)
    xr, xi = x_hat[:half], x_hat[half:]
    gr, gi = g_hat[:half], g_hat[half:]
    kr, ki = k_hat[:half], k_hat[half:]
    y_hat = jnp.concatenate([kr * xr - ki * xi, kr * xi + ki * xr], axis=0)
    h_hat = jnp.concatenate([kr * gr + ki * gi, kr * gi - ki * gr], axis=0)
    lag = jnp.concatenate([gr * xr + gi * xi, gr * xi - gi * xr], axis=0) * (1.0 / half)
    inv_both = jnp.concatenate([inv_high, inv_low], axis=1)
    outs = []
    for hat in (y_hat, h_hat):
        hat_high, hat_low = split(hat)
        outs.append(mul(inv_both, twice(hat_high, 0)) + mul(inv_high, hat_low))
    terms_high, terms_low = split(jnp.concatenate([phi_t, psi_t], axis=0))
    lag_high, lag_low = split(lag)
    wide = mul(jnp.concatenate([terms_high, terms_low], 1), twice(lag_high, 0)) + mul(
        terms_high, lag_low
    )
    return outs + [own_rows(wide[:gm], modes, group), own_rows(wide[gm:], modes, group)]


def carry_block(group, table, start):
    high, low = split(table)
    start_high, start_low = split(spread(start, table.shape[1], group))
    return mul(jnp.concatenate([high, low], 1), twice(start_high, 0)) + mul(high, start_low)


def remote(source, target, sems, k, axis, peer):
    return pltpu.make_async_remote_copy(
        src_ref=source, dst_ref=target, send_sem=sems[0].at[k], recv_sem=sems[1].at[k],
        device_id={axis: peer}, device_id_type=MESH,
    )


def whole_kernel(
    n, rows, norm, modes, group, steps,
    rate_ref, pole_ref, gap_ref, dft_ref, inv_high_ref, inv_low_ref, angle_ref, x_ref, g_ref,
    res_ref, rates_ref, state_ref, weighted_ref,
    y_ref, gs_ref, gres_ref, grate_ref,
    inbox, outbox, landed, y_held, gs_held, sum_held, moment_held, rate_held,
    sumbox, ratebox, rowbox, rowrate, gathered, *sems,
):
    step = pl.program_id(0)
    sub = rate_ref.shape[0]
    length = x_ref.shape[0]
    channels = res_ref.shape[1]
    span = sub * LANES
    me = lax.axis_index("seq")
    mine = lax.axis_index("batch")
    width = channels // n
    others = [lax.rem(me + k, n) for k in range(1, n)]
    beside = [lax.rem(mine + k, rows) for k in range(1, rows)]
    pairs = [(sems[2 * i], sems[2 * i + 1]) for i in range(7)]

    def lanes(index):
        return pl.ds(pl.multiple_of(index * width, 128), width)

    def first():
        return [
            remote(state_ref.at[:, :, lanes(p)], inbox.at[me], pairs[0], k, "seq", p)
            for k, p in enumerate(others)
        ]

    def second():
        return [
            remote(outbox.at[p], landed.at[:, :, lanes(me)], pairs[1], k, "seq", p)
            for k, p in enumerate(others)
        ]

    def third():
        return [
            remote(sum_held.at[:, lanes(p)], sumbox.at[me], pairs[2], k, "seq", p)
            for k, p in enumerate(others)
        ] + [
            remote(rate_held, ratebox.at[me], pairs[3], k, "seq", p) for k, p in enumerate(others)
        ]

    def fourth():
        return [
            remote(rowbox.at[mine], rowbox.at[mine], pairs[4], k, "batch", p)
            for k, p in enumerate(beside)
        ] + [
            remote(rowrate.at[mine], rowrate.at[mine], pairs[5], k, "batch", p)
            for k, p in enumerate(beside)
        ]

    def fifth():
        return [
            remote(gathered.at[:, lanes(me)], gathered.at[:, lanes(me)], pairs[6], k, "seq", p)
            for k, p in enumerate(others)
        ]

    @pl.when(step == 0)
    def _():
        barrier = pltpu.get_barrier_semaphore()
        for p in others:
            pl.semaphore_signal(barrier, inc=1, device_id={"seq": p}, device_id_type=MESH)
        for p in beside:
            pl.semaphore_signal(barrier, inc=1, device_id={"batch": p}, device_id_type=MESH)
        pl.semaphore_wait(barrier, len(others) + len(beside))
        for copy in first():
            copy.start()

    @pl.when(step == steps // 2)
    def _():
        for copy in first():
            copy.wait_recv()
        inbox[me] = state_ref[:, :, lanes(me)]
        whole = jnp.exp(-rates_ref[:, lanes(me)] * float(length))
        carry = jnp.zeros_like(whole)
        adjoint = jnp.zeros_like(whole)
        for i in range(n):
            outbox[i, 0] = carry
            carry = inbox[i, 0] + whole * carry
            last = n - 1 - i
            outbox[last, 1] = adjoint
            adjoint = inbox[last, 1] + whole * adjoint
        for copy in second():
            copy.start()
        landed[:, :, lanes(me)] = outbox[me]

    @pl.when(step < steps)
    def _():
        for j in range(sub):
            here = slice(j * LANES, (j + 1) * LANES)
            at = pl.ds(pl.multiple_of(step * span + j * LANES, 128), LANES)
            y, gs, sums, moments = nega_block(
                modes, group, pole_ref[j], gap_ref[j], dft_ref[...], inv_high_ref[...],
                inv_low_ref[...], angle_ref[...], x_ref[:, here], g_ref[:, here], res_ref[:, at],
            )
            y_held[:, at] = y
            gs_held[:, at] = gs
            sum_held[:, at] = sums
            moment_held[:, at] = moments

    @pl.when(step == steps)
    def _():
        for copy in second():
            copy.wait_recv()
        per = LANES // group
        many = 128 // per
        row_id = lax.broadcasted_iota(jnp.int32, (LANES, 128), 0) // group
        col_id = lax.broadcasted_iota(jnp.int32, (LANES, 128), 1)

        def lap(c, nothing):
            added = jnp.zeros((2 * modes, 128), F32)
            for j in range(many):
                at = pl.ds(pl.multiple_of((c * many + j) * LANES, 128), LANES)
                rate = rates_ref[:, at]
                pole = jnp.exp(-rate)
                whole = jnp.exp(-rate * float(length))
                fold = 1.0 / (1.0 + whole)
                s_x, s_g = state_ref[0, :, at], state_ref[1, :, at]
                carry, adjoint = landed[0, :, at], landed[1, :, at]
                turned_x, turned_g = s_x * fold, s_g * fold
                carry_all, adjoint_all = carry + turned_x, adjoint + turned_g
                res = res_ref[:, at]
                sum_held[:, at] = sum_held[:, at] + carry_all * pole * s_g
                moments = (
                    moment_held[:, at]
                    + pole * (carry_all * weighted_ref[1, :, at] + adjoint_all * weighted_ref[0, :, at])
                    + float(length) * pole * whole * (carry * adjoint - turned_x * turned_g)
                )
                landed[0, :, at] = res * carry_all
                landed[1, :, at] = res * adjoint_all
                pick = jnp.where(row_id + j * per == col_id, 1.0, 0.0).astype(BF16)
                added += mul(jnp.concatenate(split(-rate * res * moments), 0), pick)
            rate_held[:, pl.ds(pl.multiple_of(c * 128, 128), 128)] = added[:modes] + added[modes:]
            return nothing

        lax.fori_loop(0, channels // (LANES * many), lap, 0)
        for copy in third():
            copy.start()
        sumbox[me] = sum_held[:, lanes(me)]
        ratebox[me] = rate_held[...]

    @pl.when(step >= steps)
    def _():
        for j in range(sub):
            here = slice(j * LANES, (j + 1) * LANES)
            at = pl.ds(pl.multiple_of((step - steps) * span + j * LANES, 128), LANES)
            rate = rate_ref[j]
            when = lax.broadcasted_iota(jnp.int32, (length, rate.shape[1]), 0).astype(F32)
            rising = jnp.exp(-rate * (when + 1.0))
            falling = jnp.exp(-rate * (length - when))
            y = y_held[:, at] + carry_block(group, rising, landed[0, :, at])
            y_ref[:, here] = y.astype(BF16)
            gs = gs_held[:, at] + carry_block(group, falling, landed[1, :, at])
            gs_ref[:, here] = gs.astype(BF16)

    @pl.when(step == 2 * steps - 1)
    def _():
        for copy in third():
            copy.wait_recv()
        part, rate_part = sumbox[0], ratebox[0]
        for i in range(1, n):
            part = part + sumbox[i]
            rate_part = rate_part + ratebox[i]
        rowbox[mine] = part
        rowrate[mine] = rate_part
        for copy in fourth():
            copy.start()
        for copy in fourth():
            copy.wait_recv()
        part, rate_part = rowbox[0], rowrate[0]
        for i in range(1, rows):
            part = part + rowbox[i]
            rate_part = rate_part + rowrate[i]
        gathered[:, lanes(me)] = part * norm
        for copy in fifth():
            copy.start()
        grate_ref[...] = rate_part * norm
        for copy in fifth():
            copy.wait_recv()
        gres_ref[...] = gathered[...]
        for copy in first() + second() + third() + fourth() + fifth():
            copy.wait_send()


def constants(length):
    half = length // 2
    omega = np.pi * (2.0 * np.arange(half) + 1.0) / length
    at = np.arange(length)
    forward = np.concatenate([np.cos(np.outer(omega, at)), -np.sin(np.outer(omega, at))], axis=0)
    lanes = np.ones((1, 128))
    angle = np.stack(
        [2.0 * np.sin(omega / 2.0)[:, None] ** 2 * lanes, np.sin(omega)[:, None] * lanes]
    )
    return forward.astype(np.float32), (forward.T / half).astype(np.float32), angle.astype(np.float32)


def local(mesh_shape, signal, out_grad, residues, log_rates):
    batch_rows, length, channels = signal.shape
    modes, groups = log_rates.shape
    group = channels // groups
    blocks = channels // LANES
    gm = LANES // group * modes
    norm = 1.0 / (batch_rows * mesh_shape["batch"] * length * mesh_shape["seq"])
    decay = jnp.exp(log_rates)
    flat = decay.T.reshape(blocks, 1, gm)
    pole = jnp.exp(-flat)
    gap = -jnp.expm1(-flat)
    lane_rate = jnp.repeat(decay, group, axis=1)
    forward, inverse, angle = constants(length)
    dft_high = jnp.asarray(forward).astype(BF16)
    dft = jnp.concatenate(
        [dft_high, (jnp.asarray(forward) - dft_high.astype(F32)).astype(BF16)], axis=1
    )
    inv_high, inv_low = split(jnp.asarray(inverse))
    angle = jnp.asarray(angle)
    peers, rows = mesh_shape["seq"], mesh_shape["batch"]
    width = channels // peers

    def specs(sub):
        return (
            pl.BlockSpec((sub, 1, gm), lambda b: (b, 0, 0)),
            pl.BlockSpec((length, sub * LANES), lambda b: (0, b)),
            pl.BlockSpec((modes, sub * LANES), lambda b: (0, b)),
            pl.BlockSpec((2, modes, sub * LANES), lambda b: (0, 0, b)),
        )

    def fixed(shape):
        return pl.BlockSpec(shape, lambda b: (0,) * len(shape))

    def dma(count):
        return pltpu.SemaphoreType.DMA((max(count, 1),))

    pair = jax.ShapeDtypeStruct((2, modes, channels), F32)
    mixed, grads, res_sum, rate_sum = [], [], 0.0, 0.0
    for row in range(batch_rows):
        x, g = signal[row], out_grad[row]
        row_spec, data_spec, lane_spec, pair_spec = specs(STATE_SUB)
        state, weighted = pl.pallas_call(
            functools.partial(states_kernel, modes, group),
            grid=(blocks // STATE_SUB,),
            in_specs=[row_spec, data_spec, data_spec],
            out_specs=[pair_spec, pair_spec],
            out_shape=[pair, pair],
        )(flat, x, g)
        steps = blocks // MAIN_SUB
        wide = MAIN_SUB * LANES
        y, gs, part, rates = pl.pallas_call(
            functools.partial(whole_kernel, peers, rows, norm, modes, group, steps),
            grid=(2 * steps,),
            in_specs=[pl.BlockSpec((MAIN_SUB, 1, gm), lambda b: (b % steps, 0, 0))] * 3
            + [fixed(v.shape) for v in (dft, inv_high, inv_low, angle)]
            + [pl.BlockSpec((length, wide), lambda b: (0, jnp.minimum(b, steps - 1)))] * 2
            + [fixed(residues.shape), fixed(lane_rate.shape), fixed(pair.shape), fixed(pair.shape)],
            out_specs=[pl.BlockSpec((length, wide), lambda b: (0, jnp.maximum(b - steps, 0)))] * 2
            + [fixed((modes, channels)), fixed((modes, groups))],
            out_shape=[
                jax.ShapeDtypeStruct((length, channels), BF16),
                jax.ShapeDtypeStruct((length, channels), BF16),
                jax.ShapeDtypeStruct((modes, channels), F32),
                jax.ShapeDtypeStruct((modes, groups), F32),
            ],
            scratch_shapes=[
                pltpu.VMEM((peers, 2, modes, width), F32),
                pltpu.VMEM((peers, 2, modes, width), F32),
                pltpu.VMEM((2, modes, channels), F32),
                pltpu.VMEM((length, channels), F32),
                pltpu.VMEM((length, channels), F32),
                pltpu.VMEM((modes, channels), F32),
                pltpu.VMEM((modes, channels), F32),
                pltpu.VMEM((modes, groups), F32),
                pltpu.VMEM((peers, modes, width), F32),
                pltpu.VMEM((peers, modes, groups), F32),
                pltpu.VMEM((rows, modes, width), F32),
                pltpu.VMEM((rows, modes, groups), F32),
                pltpu.VMEM((modes, channels), F32),
            ]
            + [dma(peers - 1)] * 8 + [dma(rows - 1)] * 4 + [dma(peers - 1)] * 2,
            compiler_params=pltpu.CompilerParams(collective_id=0, has_side_effects=True),
        )(flat, pole, gap, dft, inv_high, inv_low, angle, x, g, residues, lane_rate, state, weighted)
        mixed.append(y)
        grads.append(gs)
        res_sum = res_sum + part if row else part
        rate_sum = rate_sum + rates if row else rates
    return jnp.stack(mixed), jnp.stack(grads), res_sum, rate_sum


def solution(mesh):
    placed = (P("batch", "seq", None), P("batch", "seq", None), P(), P())
    return jax.shard_map(
        functools.partial(local, dict(mesh.shape)),
        mesh=mesh,
        in_specs=placed,
        out_specs=placed,
        check_vma=False,
    )
```
